32 devices in a mesh: groups: 2 (over y), cells: 4 (over z), freq: 2 (over x), rep: 2 (over core).
Axes of the slice: x: 2, y: 2, z: 4, core: 2. Of those that a mesh axis runs over, the one named last changes fastest.
Arguments:
- far_adjoint: bfloat16 [16, 128, 2, 128], P(('groups', 'freq'), 'cells'), parts along dimension 0, may hold values from -6 to 6
- wavenumber: float32 [8], P('freq'), may hold values from 0.6 to 2.4
- design_params: bfloat16 [8, 131072], P(None, ('groups', 'cells', 'freq', 'rep')), parts along dimension 1, may hold values from -5 to 5
- family: int32 [256, 512], P(('groups', 'cells'), 'rep'), parts along dimension 0, may hold values from 0 to 7, as said below
- send_pick: int32 [16, 8, 1536], P(('groups', 'cells', 'rep')), parts along dimension 0, may hold values from 0 to 8192, as said below
- arrive_pick: int32 [16, 8192], P(('groups', 'cells', 'rep')), parts along dimension 0, may hold values from 0 to 12287, as said below
- input_weight: bfloat16 [8, 256, 8], replicated, may hold values from -2 to 2
- hidden_weight: bfloat16 [8, 5, 256, 256], replicated, may hold values from -0.5 to 0.5
- output_weight: bfloat16 [8, 16, 256], replicated, may hold values from -1.5 to 1.5
Outputs:
- design_gradient: float32 [8, 131072], P(None, ('groups', 'cells', 'freq', 'rep')), parts along dimension 1
The draws below stay inside these ranges and needn't reach their ends.
There are 2 independent parts, one for each index of `groups`. The reference program is written for one: setup_inputs(seed, part) draws one part's arguments, and reference() takes and returns one part's arrays. A program takes and returns all parts, laid end to end along the dimension named above; an argument that names none is the same for every part. Nothing has to cross between parts.
Inputs may be any that keep to these rules, and one draw needn't show every extreme that they name: send_pick[s, g, k] is the cell a * 256 + b (surface row (s // 2) * 32 + a, column (s % 2) * 256 + b) of surface block s that fills slot k towards sorted block g, or 8192 for an empty slot; used slots come first; every cell is sent exactly once; some pair of blocks uses all 1536 slots in every draw; every sorted block receives exactly 8192 cells. arrive_pick[g, t] = s * 1536 + k names the used slot k from surface block s towards sorted block g; each used slot is named exactly once. Along the family-sorted order families never decrease, every aligned block of 128 positions holds cells of one family, and every family occurs.
All inputs are finite; a program needn't handle non-finite values.
Results may differ from the reference program's by a relative error of at most 0.011.
Values may be sent and summed in bfloat16 or wider, within the bound.
A program may use at most 128 MiB of HBM per device.

```python
import math
import jax
import jax.numpy as jnp
from jax import lax

U = 128
V = 128
F = 8
HID = 256
P_SIZE = 8
NFAM = 8
NL = 5
BLK = 128
XD = 32
YD = 256
XSPLIT = 4
YSPLIT = 2
FSPLIT = 2
X = 128
Y = 512
CELLS = 65536
FD = 4
SHARDS = 8
QUOTA = 1024
CAP = 1536
SEG = 4096


def shared_plan(key):
    key = jax.random.fold_in(key, 7177)
    count_key, shift_key, slot_key, cell_key, family_key = jax.random.split(key, 5)
    cell_count = XD * YD
    spread = QUOTA // 8
    jitter = jax.random.randint(count_key, (SHARDS, SHARDS), -spread, spread + 1)
    jitter = jitter.at[0, 0].set(spread).at[0, 1].set(-spread).at[1, 0].set(-spread).at[1, 1].set(spread)
    mixing = jitter - jnp.roll(jitter, -1, 1) - jnp.roll(jitter, -1, 0) + jnp.roll(jnp.roll(jitter, -1, 0), -1, 1)
    column_shift = jax.random.randint(shift_key, (), 0, SHARDS)
    mixing = jnp.roll(jnp.roll(mixing, SHARDS - 1, 0), column_shift, 1)
    counts = QUOTA + mixing
    cumulative = jnp.cumsum(counts, 0)
    starts = cumulative - counts
    positions = jnp.arange(cell_count)
    labels = jnp.sum((cumulative.T[:, None, :] <= positions[None, :, None]).astype(jnp.int32), -1)
    slot_keys = jax.random.split(slot_key, SHARDS)
    permuted = jax.vmap(lambda one_key: jax.random.permutation(one_key, cell_count))(slot_keys)
    chosen_label = jnp.take_along_axis(labels, permuted, 1)
    chosen_slot = permuted - jnp.take_along_axis(starts.T, chosen_label, 1)
    arrive_pick = (chosen_label * CAP + chosen_slot).astype(jnp.int32)
    offsets = jnp.cumsum(counts, 1) - counts
    cell_keys = jax.random.split(cell_key, SHARDS)
    shuffled = jax.vmap(lambda one_key: jax.random.permutation(one_key, cell_count))(cell_keys)
    wanted = offsets[:, :, None] + jnp.arange(CAP)[None, None, :]
    valid = jnp.arange(CAP)[None, None, :] < counts[:, :, None]
    clipped = jnp.clip(wanted, 0, cell_count - 1).reshape(SHARDS, SHARDS * CAP)
    picked = jnp.take_along_axis(shuffled, clipped, 1).reshape(SHARDS, SHARDS, CAP)
    send_pick = jnp.where(valid, picked, cell_count).astype(jnp.int32)
    block_total = X * Y // BLK
    extra_kinds = jax.random.randint(family_key, (block_total - NFAM,), 0, NFAM)
    block_kinds = jnp.sort(jnp.concatenate([jnp.arange(NFAM), extra_kinds]))
    target = jnp.arange(SHARDS)[:, None]
    slot_number = jnp.arange(cell_count)[None, :]
    global_position = ((target // YSPLIT * FSPLIT + slot_number // SEG) * YSPLIT + target % YSPLIT) * SEG + slot_number % SEG
    kinds_here = block_kinds[global_position // BLK]
    local_cell = send_pick[chosen_label, target, chosen_slot]
    natural = jnp.zeros((SHARDS, cell_count), jnp.int32).at[chosen_label, local_cell].set(kinds_here)
    family = natural.reshape(XSPLIT, YSPLIT, XD, YD).transpose(0, 2, 1, 3).reshape(X, Y)
    return (send_pick, arrive_pick, family.astype(jnp.int32))


def draw_family(key, part):
    return shared_plan(key)[2]


def draw_send_pick(key, part):
    return shared_plan(key)[0]


def draw_arrive_pick(key, part):
    return shared_plan(key)[1]


def steps_of(stream_key, extent, shards, least, largest):
    def one(axis_at, blocks):
        steps = jax.random.uniform(jax.random.fold_in(jax.random.fold_in(stream_key, 6), axis_at), (blocks,), jnp.float32, least / len(shards), largest / len(shards))
        return jnp.repeat(jnp.exp(steps), extent[axis_at] // blocks).reshape((-1,) + (1,) * (len(extent) - axis_at - 1))

    factor_of = one(*shards[0])
    for cut in shards[1:]:
        factor_of = factor_of * one(*cut)
    return factor_of


def centred(rng, shape, scale, reach, shards=(), dtype=jnp.bfloat16):
    values = scale * jax.random.normal(rng, shape, jnp.float32)
    if shards:
        values = values * steps_of(rng, shape, shards, -0.22, 0.18)
    return jnp.clip(values, -reach, reach).astype(dtype)


def setup_inputs(seed: int = 0, part: int = 0) -> dict:
    splits = jax.random.split(jax.random.key(seed), 10)
    part_splits = jax.random.split(jax.random.fold_in(splits[9], part), 10)
    far_adjoint = centred(part_splits[0], (F, U, 2, V), 1.0, 6.0, ((0, 2), (1, 4)))
    wavenumber = jnp.clip(jnp.exp(math.log(2.4) - 1.3862944 * jax.random.uniform(splits[1], (F,), jnp.float32) ** steps_of(splits[1], (F,), ((0, 2),), -0.2, 0.2)), 0.6, 2.4)
    design_params = centred(part_splits[2], (P_SIZE, CELLS), 1.0, 5.0, ((1, 16),))
    family = draw_family(jax.random.fold_in(jax.random.fold_in(splits[9], part), 71), part)
    send_pick = draw_send_pick(jax.random.fold_in(jax.random.fold_in(splits[9], part), 71), part)
    arrive_pick = draw_arrive_pick(jax.random.fold_in(jax.random.fold_in(splits[9], part), 71), part)
    input_weight = centred(splits[6], (NFAM, HID, P_SIZE), P_SIZE ** -0.5, 2.0)
    hidden_weight = centred(splits[7], (NFAM, NL, HID, HID), (HID // 2) ** -0.5, 0.5)
    output_weight = centred(splits[8], (NFAM, 2 * F, HID), (2 * F) ** -0.5, 1.5)
    return {"far_adjoint": far_adjoint, "wavenumber": wavenumber, "design_params": design_params, "family": family, "send_pick": send_pick, "arrive_pick": arrive_pick, "input_weight": input_weight, "hidden_weight": hidden_weight, "output_weight": output_weight}


def phase_pair(wavenumber, direction_total, position_total, direction_start, direction_count, position_start, position_count):
    direction = (2.0 * (jnp.arange(direction_count) + direction_start).astype(jnp.float32) + 1.0) / direction_total - 1.0
    position = (jnp.arange(position_count) + position_start).astype(jnp.float32) - 0.5 * (position_total - 1)
    angles = (wavenumber * direction)[:, None] * position[None, :]
    norm_scale = 1.0 / math.sqrt(direction_total)
    return ((jnp.cos(angles) * norm_scale).astype(jnp.bfloat16), (jnp.sin(angles) * norm_scale).astype(jnp.bfloat16))

def rotation(cosine_table, sine_table):
    upper = jnp.concatenate([cosine_table, sine_table], 1)
    lower = jnp.concatenate([-sine_table, cosine_table], 1)
    return jnp.concatenate([upper, lower], 0)

def hold(values):
    return lax.optimization_barrier(values.astype(jnp.bfloat16)).astype(jnp.float32)

def silu_slope(preact):
    sigmoid = jax.nn.sigmoid(preact)
    return sigmoid * (1.0 + preact * (1.0 - sigmoid))

def cell_adjoint(far_adjoint, wavenumber):
    results = []
    for band_index in range(F):
        cosine_y, sine_y = phase_pair(wavenumber[band_index], V, Y, 0, V, 0, Y)
        cosine_x, sine_x = phase_pair(wavenumber[band_index], U, X, 0, U, 0, X)
        field_rows = far_adjoint[band_index].reshape(U, 2 * V)
        image_rows = jnp.dot(field_rows, rotation(cosine_y, sine_y), preferred_element_type=jnp.float32).astype(jnp.bfloat16)
        stacked = jnp.concatenate([image_rows[:, :Y], image_rows[:, Y:]], 0)
        left_table = rotation(cosine_x, sine_x)
        results.append(jnp.dot(left_table.T, stacked, preferred_element_type=jnp.float32).astype(jnp.bfloat16))
    return jnp.stack(results).reshape(2 * F, X, Y)

def sorted_cells(send_pick, arrive_pick):
    source = arrive_pick // CAP
    slot_index = arrive_pick % CAP
    target = jnp.arange(SHARDS)[:, None]
    local_cell = send_pick[source, target, slot_index]
    grid_row = source // YSPLIT * XD + local_cell // YD
    grid_col = source % YSPLIT * YD + local_cell % YD

    def reorder(table):
        return table.reshape(XSPLIT, YSPLIT, FSPLIT, SEG).transpose(0, 2, 1, 3).reshape(CELLS)
    return (reorder(grid_row), reorder(grid_col))

def reference(far_adjoint, wavenumber, design_params, family, send_pick, arrive_pick, input_weight, hidden_weight, output_weight):
    adjoint = cell_adjoint(far_adjoint, wavenumber)
    grid_row, grid_col = sorted_cells(send_pick, arrive_pick)
    ordered = adjoint[:, grid_row, grid_col]
    family_ids = family[grid_row, grid_col]
    segments = CELLS // SEG
    block_count = SEG // BLK

    def segment_gradient(operands):
        inputs, adjoint_rows, segment_kind = operands
        block_kind = segment_kind.reshape(block_count, BLK)[:, 0]
        first_weight = input_weight[block_kind].astype(jnp.float32)
        preact = jnp.einsum('bhp,pbr->hbr', first_weight, inputs.reshape(P_SIZE, block_count, BLK).astype(jnp.float32))
        preacts = [preact]
        for level_index in range(NL):
            activation = hold(jax.nn.silu(preact))
            weight_blocks = hidden_weight[block_kind, level_index].astype(jnp.float32)
            preact = jnp.einsum('boi,ibr->obr', weight_blocks, activation)
            preacts.append(preact)
        last_weight = output_weight[block_kind].astype(jnp.float32).reshape(block_count, FSPLIT, 2 * FD, HID)
        adjoint_blocks = adjoint_rows.reshape(FSPLIT, 2 * FD, block_count, BLK).astype(jnp.float32)
        group_parts = jnp.einsum('bgkh,gkbr->ghbr', last_weight, adjoint_blocks)
        gradient = lax.optimization_barrier(jnp.sum(hold(group_parts), 0))
        for level_index in reversed(range(NL)):
            scaled_delta = hold(gradient * silu_slope(preacts[level_index + 1]))
            weight_blocks = hidden_weight[block_kind, level_index].astype(jnp.float32)
            gradient = jnp.einsum('boi,obr->ibr', weight_blocks, scaled_delta)
        scaled_delta = hold(gradient * silu_slope(preacts[0]))
        result = jnp.einsum('bhp,hbr->pbr', first_weight, scaled_delta)
        return result.reshape(P_SIZE, SEG)
    operands = (design_params.reshape(P_SIZE, segments, SEG).transpose(1, 0, 2), ordered.reshape(2 * F, segments, SEG).transpose(1, 0, 2), family_ids.reshape(segments, SEG))
    results = lax.map(segment_gradient, operands)
    return results.transpose(1, 0, 2).reshape(P_SIZE, CELLS)
```

```python
import functools
import math

import jax
import jax.numpy as jnp
from jax import lax
from jax.experimental import pallas as pl
from jax.experimental.pallas import tpu as pltpu
from jax.sharding import PartitionSpec as P

U = 128
V = 128
HID = 256
NL = 5
BLK = 128
NFAM = 8
SUB = 8
CHUNK = 1024
LATE = 1


def one_hot_pick(table, index, width):
    count = index.shape[1]
    low = jnp.bitwise_and(index, width - 1).astype(jnp.float32).astype(jnp.bfloat16)
    high = jnp.right_shift(index, width.bit_length() - 1)
    level = lax.broadcasted_iota(jnp.int32, (width, count), 0)
    level = level.astype(jnp.float32).astype(jnp.bfloat16)
    one, zero = jnp.ones((), jnp.bfloat16), jnp.zeros((), jnp.bfloat16)
    chosen = jnp.where(level == jnp.broadcast_to(low, level.shape), one, zero)
    spread = jnp.dot(table, chosen, preferred_element_type=jnp.float32)
    high = jnp.broadcast_to(high, (SUB, count))
    total = jnp.zeros((SUB, count), jnp.float32)
    for step in range(table.shape[0] // SUB):
        total = jnp.where(high == step, spread[step * SUB : (step + 1) * SUB], total)
    return total


def row_order(pair_rows, row_count):
    shape = (row_count * SUB, pair_rows * row_count)
    target = lax.broadcasted_iota(jnp.int32, shape, 0)
    source = lax.broadcasted_iota(jnp.int32, shape, 1)
    wanted = (target % SUB) * row_count + target // SUB
    hit = jnp.logical_and(wanted == source, target % SUB < pair_rows)
    return jnp.where(hit, 1.0, 0.0).astype(jnp.bfloat16)


def angles_of(wavenumber, direction, position):
    return (wavenumber * direction) * position


def fill_right_tables(right_ref, wave_ref, column_start, column_count, column_total):
    group = 16
    scale = 1.0 / math.sqrt(V)
    for band in range(right_ref.shape[0]):
        wavenumber = wave_ref[band]
        for start in range(0, column_count, 128):
            column = lax.broadcasted_iota(jnp.int32, (group, 128), 1) + (column_start + start)
            position = column.astype(jnp.float32) - 0.5 * (column_total - 1)
            row = lax.broadcasted_iota(jnp.int32, (group, 128), 0).astype(jnp.float32)
            angle = angles_of(wavenumber, (2.0 * row + 1.0) / V - 1.0, position)
            cosine, sine = jnp.cos(angle) * scale, jnp.sin(angle) * scale
            turn = angles_of(wavenumber, 2.0 * group / V, position[:8])
            turn_cos, turn_sin = jnp.cos(turn), jnp.sin(turn)
            turn_cos = jnp.concatenate([turn_cos, turn_cos], 0)
            turn_sin = jnp.concatenate([turn_sin, turn_sin], 0)
            for low in range(0, V, group):
                at = pl.ds(low, group)
                right_ref[band, at, pl.ds(start, 128)] = cosine.astype(jnp.bfloat16)
                right_ref[band, at, pl.ds(column_count + start, 128)] = sine.astype(jnp.bfloat16)
                cosine, sine = (
                    cosine * turn_cos - sine * turn_sin,
                    sine * turn_cos + cosine * turn_sin,
                )


def fill_left_tables(left_ref, wave_ref, row_start, row_count, rows_total):
    scale = 1.0 / math.sqrt(U)
    shape = (row_count, 2 * U)
    row = lax.broadcasted_iota(jnp.int32, shape, 0) + row_start
    position = row.astype(jnp.float32) - 0.5 * (rows_total - 1)
    lane = lax.broadcasted_iota(jnp.int32, shape, 1)
    direction = (2.0 * (lane // 2).astype(jnp.float32) + 1.0) / U - 1.0
    real = lane % 2 == 0
    for band in range(left_ref.shape[0]):
        angle = angles_of(wave_ref[band], direction, position)
        cosine, sine = jnp.cos(angle) * scale, jnp.sin(angle) * scale
        upper = jnp.where(real, cosine, -sine).astype(jnp.bfloat16)
        lower = jnp.where(real, sine, cosine).astype(jnp.bfloat16)
        left_ref[band, :row_count, : 2 * U] = upper
        left_ref[band, row_count:, : 2 * U] = lower
        left_ref[band, :row_count, 2 * U :] = -lower
        left_ref[band, row_count:, 2 * U :] = upper


def nt_dot(left, right):
    return lax.dot_general(
        left, right, (((1,), (1,)), ((), ())), preferred_element_type=jnp.float32
    )


def tn_dot(left, right):
    return lax.dot_general(
        left, right, (((0,), (0,)), ((), ())), preferred_element_type=jnp.float32
    )


def blocks_of(chunk, kind_ref):
    first = chunk * (CHUNK // BLK)
    return [
        (
            pl.ds(pl.multiple_of((first + i) * BLK, BLK), BLK),
            jnp.clip(kind_ref[0, first + i], 0, NFAM - 1),
        )
        for i in range(CHUNK // BLK)
    ]


def forward_chunk(chunk, kind_ref, inputs_ref, first_ref, hidden_ref, slope_ref):
    half = jnp.asarray(0.5, jnp.bfloat16)
    blocks = blocks_of(chunk, kind_ref)
    preacts = [tn_dot(inputs_ref[:, at] * half, first_ref[kind]) for at, kind in blocks]
    for level in range(NL + 1):
        for place, (at, kind) in enumerate(blocks):
            above = 1.0 + jnp.tanh(preacts[place])
            active = preacts[place] * above
            slope_ref[level, at] = (above + active * (2.0 - above)).astype(jnp.bfloat16)
            if level < NL:
                preacts[place] = nt_dot(active.astype(jnp.bfloat16) * half, hidden_ref[kind, level])


def backward_chunk(chunk, kind_ref, ordered_ref, first_ref, hidden_ref, last_ref, slope_ref, out_ref):
    blocks = blocks_of(chunk, kind_ref)

    def delta_of(level, place, at):
        slope = slope_ref[level, at].astype(jnp.float32)
        return (gradients[place] * slope).astype(jnp.bfloat16)

    gradients = [tn_dot(ordered_ref[:, at], last_ref[kind]) for at, kind in blocks]
    for level in reversed(range(NL)):
        for place, (at, kind) in enumerate(blocks):
            gradients[place] = jnp.dot(
                delta_of(level + 1, place, at),
                hidden_ref[kind, level],
                preferred_element_type=jnp.float32,
            )
    for place, (at, kind) in enumerate(blocks):
        out_ref[:, at] = nt_dot(first_ref[kind], delta_of(0, place, at)) * (0.5 ** (NL + 1))


def fused_kernel(
    wave_hbm,
    far_ref,
    family_hbm,
    send_hbm,
    arrive_hbm,
    inputs_hbm,
    first_hbm,
    hidden_hbm,
    last_hbm,
    out_hbm,
    wave_ref,
    family_ref,
    send_ref,
    arrive_ref,
    inputs_ref,
    first_ref,
    hidden_ref,
    last_ref,
    load_sem,
    field_ref,
    right_ref,
    left_ref,
    cells_ref,
    table_ref,
    outbox_ref,
    got_ref,
    gather_ref,
    half_ref,
    ordered_ref,
    count_ref,
    counts_ref,
    kind_vmem,
    kind_ref,
    slope_ref,
    result_ref,
    far_send,
    far_recv,
    pass_send,
    pass_recv,
    count_send,
    count_recv,
    out_send,
    out_recv,
    half_send,
    half_recv,
    result_sem,
    *,
    width,
):
    n_cells, n_rep, n_freq = (lax.axis_size(name) for name in ("cells", "rep", "freq"))
    z, core, freq = (lax.axis_index(name) for name in ("cells", "rep", "freq"))
    shards = n_cells * n_rep
    me = z * n_rep + core
    bands = far_ref.shape[0]
    row_count, column_count = family_ref.shape
    slots = send_ref.shape[1]
    segment = ordered_ref.shape[1]
    pair_rows = 2 * bands
    share = bands // n_rep
    chunks = segment // CHUNK
    mesh_ids = pl.DeviceIdType.MESH

    def shard_id(shard):
        return {"cells": shard // n_rep, "rep": shard % n_rep}

    def partner(own, mask, count):
        other, bit = 0, 1
        while bit < count:
            mine, flip = (own // bit) % 2, (mask // bit) % 2
            other, bit = other + bit * (mine + flip - 2 * mine * flip), 2 * bit
        return other

    loads = [
        pltpu.make_async_copy(source, target, load_sem.at[place])
        for place, (source, target) in enumerate(
            (
                (wave_hbm, wave_ref),
                (family_hbm, family_ref),
                (far_ref, field_ref.at[z]),
                (send_hbm, send_ref),
                (inputs_hbm, inputs_ref),
                (first_hbm, first_ref),
                (hidden_hbm, hidden_ref),
                (last_hbm, last_ref),
                (arrive_hbm, arrive_ref),
            )
        )
    ]
    for load in loads[:2]:
        load.start()

    barrier = pltpu.get_barrier_semaphore()

    @pl.loop(1, shards)
    def _(step):
        pl.semaphore_signal(
            barrier, inc=1, device_id=shard_id((me + step) % shards), device_id_type=mesh_ids
        )

    @pl.loop(1, n_freq)
    def _(step):
        pl.semaphore_signal(
            barrier, inc=1, device_id={"freq": (freq + step) % n_freq}, device_id_type=mesh_ids
        )

    for load in loads[2:]:
        load.start()
    for load in loads[:2]:
        load.wait()

    rows = []
    for kind in range(NFAM):
        below = jnp.where(family_ref[...] <= kind, 1.0, 0.0)
        part = jnp.sum(below, 0, keepdims=True)
        total = part[:, :128]
        for start in range(128, column_count, 128):
            total = total + part[:, start : start + 128]
        rows.append(total)
    count_ref[...] = jnp.concatenate(rows, 0)
    counts_ref[me] = count_ref[...]

    pl.semaphore_wait(barrier, shards - 1 + n_freq - 1)

    def far_copy(mask):
        mine = pl.ds(core * share, share)
        return pltpu.make_async_remote_copy(
            src_ref=far_ref.at[mine],
            dst_ref=field_ref.at[z, mine],
            send_sem=far_send.at[mask],
            recv_sem=far_recv.at[mask],
            device_id={"cells": partner(z, mask, n_cells)},
            device_id_type=mesh_ids,
        )

    def far_arrival(mask):
        mine = pl.ds(core * share, share)
        source = partner(z, mask, n_cells)
        return pltpu.make_async_remote_copy(
            src_ref=far_ref.at[mine],
            dst_ref=field_ref.at[source, mine],
            send_sem=far_send.at[mask],
            recv_sem=far_recv.at[mask],
            device_id={"cells": source},
            device_id_type=mesh_ids,
        )

    def pass_copy(mask, lane):
        mine = pl.ds(lane * share, share)
        source = partner(z, mask, n_cells)
        return pltpu.make_async_remote_copy(
            src_ref=field_ref.at[source, mine],
            dst_ref=field_ref.at[source, mine],
            send_sem=pass_send.at[mask],
            recv_sem=pass_recv.at[mask],
            device_id={"rep": 1 - core},
            device_id_type=mesh_ids,
        )

    def count_copy(step, shard, slot):
        return pltpu.make_async_remote_copy(
            src_ref=count_ref,
            dst_ref=counts_ref.at[slot],
            send_sem=count_send.at[step],
            recv_sem=count_recv.at[slot],
            device_id=shard_id(shard),
            device_id_type=mesh_ids,
        )

    @pl.loop(1, shards)
    def _(step):
        count_copy(step, (me + step) % shards, me).start()

    for mask in reversed(range(1, n_cells)):
        far_copy(mask).start()

    fill_right_tables(right_ref, wave_ref, core * column_count, column_count, column_count * n_rep)
    fill_left_tables(left_ref, wave_ref, z * row_count, row_count, row_count * n_cells)

    for load in loads[2:]:
        load.wait()

    @pl.loop(1, shards)
    def _(step):
        count_copy(step, (me + step) % shards, (me + step) % shards).wait_recv()

    upto = jnp.sum(jnp.sum(counts_ref[...], 0), 1, keepdims=True)
    owner = (z * n_freq + freq) * n_rep + core
    block = lax.broadcasted_iota(jnp.int32, (NFAM, 128), 1)
    level = lax.broadcasted_iota(jnp.int32, (NFAM, 128), 0)
    position = (owner * segment + block * BLK).astype(jnp.float32)
    past = jnp.where(jnp.logical_and(position >= upto, level < NFAM - 1), 1.0, 0.0)
    kind_vmem[...] = jnp.sum(past, 0, keepdims=True).astype(jnp.int32)
    kind_load = pltpu.make_async_copy(kind_vmem, kind_ref, load_sem.at[len(loads)])
    kind_load.start()
    kind_load.wait()

    def forward(chunk):
        forward_chunk(chunk, kind_ref, inputs_ref, first_ref, hidden_ref, slope_ref)

    early = min(chunks - LATE, n_cells - 1)

    @pl.loop(1, early + 1)
    def _(mask):
        far_arrival(mask).wait_recv()
        pass_copy(mask, core).start()
        forward(mask - 1)

    for mask in range(early + 1, n_cells):
        far_arrival(mask).wait_recv()
        pass_copy(mask, core).start()
    for mask in range(1, n_cells):
        pass_copy(mask, 1 - core).wait_recv()

    for band in range(bands):
        field = field_ref[:, band].reshape(2 * U, V)
        image = jnp.dot(field, right_ref[band], preferred_element_type=jnp.float32).astype(
            jnp.bfloat16
        )
        stacked = jnp.concatenate([image[:, :column_count], image[:, column_count:]], 0)
        cells_ref[band * 2 * row_count : (band + 1) * 2 * row_count] = jnp.dot(
            left_ref[band], stacked, preferred_element_type=jnp.float32
        ).astype(jnp.bfloat16)
    table_ref[...] = jnp.dot(
        row_order(pair_rows, row_count), cells_ref[...], preferred_element_type=jnp.float32
    ).astype(jnp.bfloat16)

    def out_copy(shard, slot):
        return pltpu.make_async_remote_copy(
            src_ref=outbox_ref.at[shard],
            dst_ref=got_ref.at[slot],
            send_sem=out_send.at[shard],
            recv_sem=out_recv.at[slot],
            device_id=shard_id(shard),
            device_id_type=mesh_ids,
        )

    grain = 384

    @pl.loop(1, shards)
    def _(step):
        shard = partner(me, shards - step, shards)
        for start in range(0, slots, grain):
            at = pl.ds(start, grain)
            picked = one_hot_pick(table_ref[...], send_ref[pl.ds(shard, 1), at], column_count)
            outbox_ref[shard, :, at] = picked.astype(jnp.bfloat16)
        out_copy(shard, me).start()

    for start in range(0, slots, grain):
        at = pl.ds(start, grain)
        picked = one_hot_pick(table_ref[...], send_ref[pl.ds(me, 1), at], column_count)
        got_ref[me, :, at] = picked.astype(jnp.bfloat16)

    pl.loop(early, chunks)(forward)

    @pl.loop(1, shards)
    def _(step):
        shard = (me + step) % shards
        out_copy(shard, shard).wait_recv()

    per_shard = slots // width
    for shard in range(shards):
        for part in range(per_shard):
            row = (shard * per_shard + part) * SUB
            gather_ref[row : row + SUB] = got_ref[
                shard, :, part * width : (part + 1) * width
            ].astype(jnp.float32)
    gathered = gather_ref[...].astype(jnp.bfloat16)

    def half_copy(step, slot, chunk):
        at = pl.ds(pl.multiple_of(chunk * CHUNK, CHUNK), CHUNK)
        return pltpu.make_async_remote_copy(
            src_ref=half_ref.at[0, step, :, at],
            dst_ref=half_ref.at[1, slot, :, at],
            send_sem=half_send.at[step, chunk],
            recv_sem=half_recv.at[slot, chunk],
            device_id={"freq": (freq + step) % n_freq},
            device_id_type=mesh_ids,
        )

    piece = 512

    def pick_half(target, chunk, side, slot):
        for start in range(chunk * CHUNK, (chunk + 1) * CHUNK, piece):
            at = pl.ds(pl.multiple_of(target * segment + start, piece), piece)
            half_ref[side, slot, :, pl.ds(start, piece)] = one_hot_pick(
                gathered, arrive_ref[:, at], width
            ).astype(jnp.bfloat16)

    @pl.loop(1, n_freq)
    def _(step):
        for chunk in range(chunks):
            pick_half((freq + step) % n_freq, chunk, 0, step)
            half_copy(step, freq, chunk).start()

    for chunk in range(chunks):
        pick_half(freq, chunk, 1, freq)

    def columns(chunk):
        return pl.ds(pl.multiple_of(chunk * CHUNK, CHUNK), CHUNK)

    def result_copy(chunk):
        return pltpu.make_async_copy(
            result_ref.at[:, columns(chunk)], out_hbm.at[:, columns(chunk)], result_sem.at[chunk]
        )

    @pl.loop(0, chunks)
    def _(chunk):
        @pl.loop(1, n_freq)
        def _(step):
            half_copy(step, (freq + step) % n_freq, chunk).wait_recv()

        for group in range(n_freq):
            ordered_ref[group * SUB : (group + 1) * SUB, columns(chunk)] = half_ref[
                1, group, :, columns(chunk)
            ]
        backward_chunk(
            chunk, kind_ref, ordered_ref, first_ref, hidden_ref, last_ref, slope_ref, result_ref
        )
        result_copy(chunk).start()

    for mask in range(1, n_cells):
        far_copy(mask).wait_send()
        pass_copy(mask, core).wait_send()

    @pl.loop(1, shards)
    def _(step):
        count_copy(step, (me + step) % shards, me).wait_send()
        out_copy((me + step) % shards, me).wait_send()

    @pl.loop(1, n_freq)
    def _(step):
        for chunk in range(chunks):
            half_copy(step, freq, chunk).wait_send()

    for chunk in range(chunks):
        result_copy(chunk).wait()


def far_memory(count):
    return [pl.BlockSpec(memory_space=pltpu.HBM)] * count


def per_device(
    far_adjoint,
    wavenumber,
    design_params,
    family,
    send_pick,
    arrive_pick,
    input_weight,
    hidden_weight,
    output_weight,
):
    row_count, column_count = family.shape
    cell_count = row_count * column_count
    bands = far_adjoint.shape[0]
    band_groups = lax.axis_size("freq")
    segment = cell_count // band_groups
    chunks = segment // CHUNK
    pair_rows = 2 * bands
    shards, slots = send_pick.shape[1:]
    directions = far_adjoint.shape[1]
    n_cells = lax.axis_size("cells")
    width = 256 if slots % 256 == 0 else 128
    bf16, dma = jnp.bfloat16, pltpu.SemaphoreType.DMA
    last_weight = output_weight.reshape(NFAM, band_groups, pair_rows, HID)
    last_weight = jnp.pad(last_weight, ((0, 0), (0, 0), (0, SUB - pair_rows), (0, 0)))
    last_weight = last_weight.reshape(NFAM, band_groups * SUB, HID)
    input_weight = jnp.swapaxes(input_weight, 1, 2)
    return pl.pallas_call(
        functools.partial(fused_kernel, width=width),
        out_shape=jax.ShapeDtypeStruct(design_params.shape, jnp.float32),
        in_specs=far_memory(9),
        out_specs=pl.BlockSpec(memory_space=pltpu.HBM),
        scratch_shapes=[
            pltpu.SMEM(wavenumber.shape, jnp.float32),
            pltpu.VMEM(family.shape, jnp.int32),
            pltpu.VMEM((shards, slots), jnp.int32),
            pltpu.VMEM(arrive_pick.shape, jnp.int32),
            pltpu.VMEM(design_params.shape, bf16),
            pltpu.VMEM(input_weight.shape, bf16),
            pltpu.VMEM(hidden_weight.shape, bf16),
            pltpu.VMEM(last_weight.shape, bf16),
            dma((10,)),
            pltpu.VMEM((n_cells, bands, 2 * directions, V), bf16),
            pltpu.VMEM((bands, V, 2 * column_count), bf16),
            pltpu.VMEM((bands, 2 * row_count, 4 * U), bf16),
            pltpu.VMEM((pair_rows * row_count, column_count), bf16),
            pltpu.VMEM((row_count * SUB, column_count), bf16),
            pltpu.VMEM((shards, SUB, slots), bf16),
            pltpu.VMEM((shards, SUB, slots), bf16),
            pltpu.VMEM((shards * slots // width * SUB, width), jnp.float32),
            pltpu.VMEM((2, band_groups, SUB, segment), bf16),
            pltpu.VMEM((band_groups * SUB, segment), bf16),
            pltpu.VMEM((NFAM, 128), jnp.float32),
            pltpu.VMEM((shards, NFAM, 128), jnp.float32),
            pltpu.VMEM((1, 128), jnp.int32),
            pltpu.SMEM((1, 128), jnp.int32),
            pltpu.VMEM((NL + 1, segment, HID), bf16),
            pltpu.VMEM(design_params.shape, jnp.float32),
            dma((n_cells,)),
            dma((n_cells,)),
            dma((n_cells,)),
            dma((n_cells,)),
            dma((shards,)),
            dma((shards,)),
            dma((shards,)),
            dma((shards,)),
            dma((band_groups, chunks)),
            dma((band_groups, chunks)),
            dma((chunks,)),
        ],
        compiler_params=pltpu.CompilerParams(
            collective_id=0, has_side_effects=True, vmem_limit_bytes=62 << 20
        ),
        name="fused",
    )(
        wavenumber,
        far_adjoint.reshape(bands, 2 * directions, V),
        family,
        send_pick.reshape(shards, slots),
        arrive_pick,
        design_params,
        input_weight,
        hidden_weight,
        last_weight,
    )


def solution(mesh):
    return jax.shard_map(
        per_device,
        mesh=mesh,
        in_specs=(
            P(("groups", "freq"), "cells", None, None),
            P("freq"),
            P(None, ("groups", "cells", "freq", "rep")),
            P(("groups", "cells"), "rep"),
            P(("groups", "cells", "rep"), None, None),
            P(("groups", "cells", "rep"), None),
            P(),
            P(),
            P(),
        ),
        out_specs=P(None, ("groups", "cells", "freq", "rep")),
        check_vma=False,
    )
```

```python
import functools
import math

import jax
import jax.numpy as jnp
from jax import lax
from jax.experimental import pallas as pl
from jax.experimental.pallas import tpu as pltpu
from jax.sharding import PartitionSpec as P

U = 128
V = 128
HID = 256
NL = 5
BLK = 128
NFAM = 8
SUB = 8
CHUNK = 1024
GRAIN = 512


def one_hot_pick(table, index, width):
    count = index.shape[1]
    low = jnp.bitwise_and(index, width - 1).astype(jnp.float32).astype(jnp.bfloat16)
    high = jnp.right_shift(index, width.bit_length() - 1)
    level = lax.broadcasted_iota(jnp.int32, (width, count), 0)
    level = level.astype(jnp.float32).astype(jnp.bfloat16)
    one, zero = jnp.ones((), jnp.bfloat16), jnp.zeros((), jnp.bfloat16)
    chosen = jnp.where(level == jnp.broadcast_to(low, level.shape), one, zero)
    spread = jnp.dot(table, chosen, preferred_element_type=jnp.float32)
    high = jnp.broadcast_to(high, (SUB, count))
    total = jnp.zeros((SUB, count), jnp.float32)
    for step in range(table.shape[0] // SUB):
        total = jnp.where(high == step, spread[step * SUB : (step + 1) * SUB], total)
    return total


def row_order(pair_rows, row_count):
    shape = (row_count * SUB, pair_rows * row_count)
    target = lax.broadcasted_iota(jnp.int32, shape, 0)
    source = lax.broadcasted_iota(jnp.int32, shape, 1)
    wanted = (target % SUB) * row_count + target // SUB
    hit = jnp.logical_and(wanted == source, target % SUB < pair_rows)
    return jnp.where(hit, 1.0, 0.0).astype(jnp.bfloat16)


def angles_of(wavenumber, direction, position):
    return (wavenumber * direction) * position


def fill_right_tables(right_ref, wave_ref, column_start, column_count, column_total):
    group = 16
    scale = 1.0 / math.sqrt(V)
    for band in range(right_ref.shape[0]):
        wavenumber = wave_ref[band]
        for start in range(0, column_count, 128):
            column = lax.broadcasted_iota(jnp.int32, (group, 128), 1) + (column_start + start)
            position = column.astype(jnp.float32) - 0.5 * (column_total - 1)
            row = lax.broadcasted_iota(jnp.int32, (group, 128), 0).astype(jnp.float32)
            angle = angles_of(wavenumber, (2.0 * row + 1.0) / V - 1.0, position)
            cosine, sine = jnp.cos(angle) * scale, jnp.sin(angle) * scale
            turn = angles_of(wavenumber, 2.0 * group / V, position[:8])
            turn_cos, turn_sin = jnp.cos(turn), jnp.sin(turn)
            turn_cos = jnp.concatenate([turn_cos, turn_cos], 0)
            turn_sin = jnp.concatenate([turn_sin, turn_sin], 0)
            for low in range(0, V, group):
                at = pl.ds(low, group)
                right_ref[band, at, pl.ds(start, 128)] = cosine.astype(jnp.bfloat16)
                right_ref[band, at, pl.ds(column_count + start, 128)] = sine.astype(jnp.bfloat16)
                cosine, sine = (
                    cosine * turn_cos - sine * turn_sin,
                    sine * turn_cos + cosine * turn_sin,
                )


def fill_left_tables(left_ref, wave_ref, row_start, row_count, rows_total):
    scale = 1.0 / math.sqrt(U)
    shape = (row_count, 2 * U)
    row = lax.broadcasted_iota(jnp.int32, shape, 0) + row_start
    position = row.astype(jnp.float32) - 0.5 * (rows_total - 1)
    lane = lax.broadcasted_iota(jnp.int32, shape, 1)
    direction = (2.0 * (lane // 2).astype(jnp.float32) + 1.0) / U - 1.0
    real = lane % 2 == 0
    for band in range(left_ref.shape[0]):
        angle = angles_of(wave_ref[band], direction, position)
        cosine, sine = jnp.cos(angle) * scale, jnp.sin(angle) * scale
        upper = jnp.where(real, cosine, -sine).astype(jnp.bfloat16)
        lower = jnp.where(real, sine, cosine).astype(jnp.bfloat16)
        left_ref[band, :row_count, : 2 * U] = upper
        left_ref[band, row_count:, : 2 * U] = lower
        left_ref[band, :row_count, 2 * U :] = -lower
        left_ref[band, row_count:, 2 * U :] = upper


def nt_dot(left, right):
    return lax.dot_general(
        left, right, (((1,), (1,)), ((), ())), preferred_element_type=jnp.float32
    )


def tn_dot(left, right):
    return lax.dot_general(
        left, right, (((0,), (0,)), ((), ())), preferred_element_type=jnp.float32
    )


def blocks_of(chunk, kind_ref):
    first = chunk * (CHUNK // BLK)
    return [
        (
            pl.ds(pl.multiple_of((first + i) * BLK, BLK), BLK),
            jnp.clip(kind_ref[0, first + i], 0, NFAM - 1),
        )
        for i in range(CHUNK // BLK)
    ]


def forward_chunk(chunk, kind_ref, inputs_ref, first_ref, hidden_ref, slope_ref):
    half = jnp.asarray(0.5, jnp.bfloat16)
    blocks = blocks_of(chunk, kind_ref)
    preacts = [tn_dot(inputs_ref[:, at] * half, first_ref[kind]) for at, kind in blocks]
    for level in range(NL + 1):
        for place, (at, kind) in enumerate(blocks):
            above = 1.0 + jnp.tanh(preacts[place])
            active = preacts[place] * above
            slope_ref[level, at] = (above + active * (2.0 - above)).astype(jnp.bfloat16)
            if level < NL:
                preacts[place] = nt_dot(active.astype(jnp.bfloat16), hidden_ref[kind, level])


def backward_chunk(chunk, kind_ref, ordered_ref, first_ref, hidden_ref, last_ref, slope_ref, out_ref):
    blocks = blocks_of(chunk, kind_ref)

    def delta_of(level, place, at):
        slope = slope_ref[level, at].astype(jnp.float32)
        return (gradients[place] * slope).astype(jnp.bfloat16)

    gradients = [tn_dot(ordered_ref[:, at], last_ref[kind]) for at, kind in blocks]
    for level in reversed(range(NL)):
        for place, (at, kind) in enumerate(blocks):
            gradients[place] = jnp.dot(
                delta_of(level + 1, place, at),
                hidden_ref[kind, level],
                preferred_element_type=jnp.float32,
            )
    for place, (at, kind) in enumerate(blocks):
        out_ref[:, at] = nt_dot(first_ref[kind], delta_of(0, place, at)) * 0.5


def fused_kernel(
    wave_hbm,
    far_ref,
    family_hbm,
    send_hbm,
    arrive_hbm,
    inputs_hbm,
    first_hbm,
    hidden_hbm,
    last_hbm,
    result_ref,
    wave_ref,
    family_ref,
    send_ref,
    arrive_ref,
    inputs_ref,
    first_ref,
    hidden_ref,
    last_ref,
    load_sem,
    field_ref,
    right_ref,
    left_ref,
    cells_ref,
    table_ref,
    outbox_ref,
    got_ref,
    gather_ref,
    half_ref,
    ordered_ref,
    count_ref,
    counts_ref,
    kind_vmem,
    kind_ref,
    slope_ref,
    far_send,
    far_recv,
    pass_send,
    pass_recv,
    count_send,
    count_recv,
    out_send,
    out_recv,
    half_send,
    half_recv,
    *,
    width,
):
    n_cells, n_rep, n_freq = (lax.axis_size(name) for name in ("cells", "rep", "freq"))
    z, core, freq = (lax.axis_index(name) for name in ("cells", "rep", "freq"))
    shards = n_cells * n_rep
    me = z * n_rep + core
    bands = far_ref.shape[0]
    row_count, column_count = family_ref.shape
    slots = send_ref.shape[1]
    segment = ordered_ref.shape[1]
    pair_rows = 2 * bands
    share = bands // n_rep
    chunks = segment // CHUNK
    mesh_ids = pl.DeviceIdType.MESH

    def shard_id(shard):
        return {"cells": shard // n_rep, "rep": shard % n_rep}

    def partner(own, mask, count):
        other, bit = 0, 1
        while bit < count:
            mine, flip = (own // bit) % 2, (mask // bit) % 2
            other, bit = other + bit * (mine + flip - 2 * mine * flip), 2 * bit
        return other

    loads = [
        pltpu.make_async_copy(source, target, load_sem.at[place])
        for place, (source, target) in enumerate(
            (
                (wave_hbm, wave_ref),
                (family_hbm, family_ref),
                (far_ref, field_ref.at[z]),
                (send_hbm, send_ref),
                (inputs_hbm, inputs_ref),
                (first_hbm, first_ref),
                (hidden_hbm, hidden_ref),
                (last_hbm, last_ref),
                (arrive_hbm, arrive_ref),
            )
        )
    ]
    for load in loads[:2]:
        load.start()

    barrier = pltpu.get_barrier_semaphore()

    @pl.loop(1, shards)
    def _(step):
        pl.semaphore_signal(
            barrier, inc=1, device_id=shard_id((me + step) % shards), device_id_type=mesh_ids
        )

    @pl.loop(1, n_freq)
    def _(step):
        pl.semaphore_signal(
            barrier, inc=1, device_id={"freq": (freq + step) % n_freq}, device_id_type=mesh_ids
        )

    for load in loads[2:]:
        load.start()
    for load in loads[:2]:
        load.wait()

    rows = []
    for kind in range(NFAM):
        below = jnp.where(family_ref[...] <= kind, 1.0, 0.0)
        part = jnp.sum(below, 0, keepdims=True)
        total = part[:, :128]
        for start in range(128, column_count, 128):
            total = total + part[:, start : start + 128]
        rows.append(total)
    count_ref[...] = jnp.concatenate(rows, 0)
    counts_ref[me] = count_ref[...]

    pl.semaphore_wait(barrier, shards - 1 + n_freq - 1)

    def far_copy(mask):
        mine = pl.ds(core * share, share)
        return pltpu.make_async_remote_copy(
            src_ref=far_ref.at[mine],
            dst_ref=field_ref.at[z, mine],
            send_sem=far_send.at[mask],
            recv_sem=far_recv.at[mask],
            device_id={"cells": partner(z, mask, n_cells)},
            device_id_type=mesh_ids,
        )

    def far_arrival(mask):
        mine = pl.ds(core * share, share)
        source = partner(z, mask, n_cells)
        return pltpu.make_async_remote_copy(
            src_ref=far_ref.at[mine],
            dst_ref=field_ref.at[source, mine],
            send_sem=far_send.at[mask],
            recv_sem=far_recv.at[mask],
            device_id={"cells": source},
            device_id_type=mesh_ids,
        )

    def pass_copy(mask, lane):
        mine = pl.ds(lane * share, share)
        source = partner(z, mask, n_cells)
        return pltpu.make_async_remote_copy(
            src_ref=field_ref.at[source, mine],
            dst_ref=field_ref.at[source, mine],
            send_sem=pass_send.at[mask],
            recv_sem=pass_recv.at[mask],
            device_id={"rep": 1 - core},
            device_id_type=mesh_ids,
        )

    def count_copy(step, shard, slot):
        return pltpu.make_async_remote_copy(
            src_ref=count_ref,
            dst_ref=counts_ref.at[slot],
            send_sem=count_send.at[step],
            recv_sem=count_recv.at[slot],
            device_id=shard_id(shard),
            device_id_type=mesh_ids,
        )

    @pl.loop(1, shards)
    def _(step):
        count_copy(step, (me + step) % shards, me).start()

    for mask in reversed(range(1, n_cells)):
        far_copy(mask).start()

    fill_right_tables(right_ref, wave_ref, core * column_count, column_count, column_count * n_rep)
    fill_left_tables(left_ref, wave_ref, z * row_count, row_count, row_count * n_cells)

    for load in loads[2:]:
        load.wait()

    @pl.loop(0, NFAM)
    def _(kind):
        for level in range(NL):
            hidden_ref[kind, level] = hidden_ref[kind, level] * jnp.asarray(0.5, jnp.bfloat16)

    @pl.loop(1, shards)
    def _(step):
        count_copy(step, (me + step) % shards, (me + step) % shards).wait_recv()

    upto = jnp.sum(jnp.sum(counts_ref[...], 0), 1, keepdims=True)
    owner = (z * n_freq + freq) * n_rep + core
    block = lax.broadcasted_iota(jnp.int32, (NFAM, 128), 1)
    level = lax.broadcasted_iota(jnp.int32, (NFAM, 128), 0)
    position = (owner * segment + block * BLK).astype(jnp.float32)
    past = jnp.where(jnp.logical_and(position >= upto, level < NFAM - 1), 1.0, 0.0)
    kind_vmem[...] = jnp.sum(past, 0, keepdims=True).astype(jnp.int32)
    kind_load = pltpu.make_async_copy(kind_vmem, kind_ref, load_sem.at[len(loads)])
    kind_load.start()
    kind_load.wait()

    def forward(chunk):
        forward_chunk(chunk, kind_ref, inputs_ref, first_ref, hidden_ref, slope_ref)

    early, last_chunks = 1, chunks // 4

    for mask in range(1, n_cells):
        far_arrival(mask).wait_recv()
        pass_copy(mask, core).start()
        if mask == 1:
            pl.loop(0, early)(forward)
    for mask in range(1, n_cells):
        pass_copy(mask, 1 - core).wait_recv()

    for band in range(bands):
        field = field_ref[:, band].reshape(2 * U, V)
        image = jnp.dot(field, right_ref[band], preferred_element_type=jnp.float32).astype(
            jnp.bfloat16
        )
        stacked = jnp.concatenate([image[:, :column_count], image[:, column_count:]], 0)
        cells_ref[band * 2 * row_count : (band + 1) * 2 * row_count] = jnp.dot(
            left_ref[band], stacked, preferred_element_type=jnp.float32
        ).astype(jnp.bfloat16)
    table_ref[...] = jnp.dot(
        row_order(pair_rows, row_count), cells_ref[...], preferred_element_type=jnp.float32
    ).astype(jnp.bfloat16)

    def out_copy(shard, slot):
        return pltpu.make_async_remote_copy(
            src_ref=outbox_ref.at[shard],
            dst_ref=got_ref.at[slot],
            send_sem=out_send.at[shard],
            recv_sem=out_recv.at[slot],
            device_id=shard_id(shard),
            device_id_type=mesh_ids,
        )

    grain = GRAIN if slots % GRAIN == 0 else slots

    @pl.loop(1, shards)
    def _(step):
        shard = partner(me, shards - step, shards)
        for start in range(0, slots, grain):
            at = pl.ds(start, grain)
            picked = one_hot_pick(table_ref[...], send_ref[pl.ds(shard, 1), at], column_count)
            outbox_ref[shard, :, at] = picked.astype(jnp.bfloat16)
        out_copy(shard, me).start()

    for start in range(0, slots, grain):
        at = pl.ds(start, grain)
        picked = one_hot_pick(table_ref[...], send_ref[pl.ds(me, 1), at], column_count)
        got_ref[me, :, at] = picked.astype(jnp.bfloat16)

    pl.loop(early, chunks - last_chunks)(forward)

    @pl.loop(1, shards)
    def _(step):
        shard = (me + step) % shards
        out_copy(shard, shard).wait_recv()

    per_shard = slots // width
    for shard in range(shards):
        for part in range(per_shard):
            row = (shard * per_shard + part) * SUB
            gather_ref[row : row + SUB] = got_ref[
                shard, :, part * width : (part + 1) * width
            ].astype(jnp.float32)
    gathered = gather_ref[...].astype(jnp.bfloat16)

    def half_copy(step, slot, chunk):
        at = pl.ds(pl.multiple_of(chunk * CHUNK, CHUNK), CHUNK)
        return pltpu.make_async_remote_copy(
            src_ref=half_ref.at[0, step, :, at],
            dst_ref=half_ref.at[1, slot, :, at],
            send_sem=half_send.at[step, chunk],
            recv_sem=half_recv.at[slot, chunk],
            device_id={"freq": (freq + step) % n_freq},
            device_id_type=mesh_ids,
        )

    piece = 512

    def pick_half(target, chunk, side, slot):
        for start in range(chunk * CHUNK, (chunk + 1) * CHUNK, piece):
            at = pl.ds(pl.multiple_of(target * segment + start, piece), piece)
            half_ref[side, slot, :, pl.ds(start, piece)] = one_hot_pick(
                gathered, arrive_ref[:, at], width
            ).astype(jnp.bfloat16)

    @pl.loop(1, n_freq)
    def _(step):
        for chunk in range(chunks):
            pick_half((freq + step) % n_freq, chunk, 0, step)
            half_copy(step, freq, chunk).start()

    for chunk in range(chunks):
        pick_half(freq, chunk, 1, freq)

    pl.loop(chunks - last_chunks, chunks)(forward)

    def columns(chunk):
        return pl.ds(pl.multiple_of(chunk * CHUNK, CHUNK), CHUNK)

    @pl.loop(0, chunks)
    def _(chunk):
        @pl.loop(1, n_freq)
        def _(step):
            half_copy(step, (freq + step) % n_freq, chunk).wait_recv()

        for group in range(n_freq):
            ordered_ref[group * SUB : (group + 1) * SUB, columns(chunk)] = half_ref[
                1, group, :, columns(chunk)
            ]
        backward_chunk(
            chunk, kind_ref, ordered_ref, first_ref, hidden_ref, last_ref, slope_ref, result_ref
        )

    for mask in range(1, n_cells):
        far_copy(mask).wait_send()
        pass_copy(mask, core).wait_send()

    @pl.loop(1, shards)
    def _(step):
        count_copy(step, (me + step) % shards, me).wait_send()
        out_copy((me + step) % shards, me).wait_send()

    @pl.loop(1, n_freq)
    def _(step):
        for chunk in range(chunks):
            half_copy(step, freq, chunk).wait_send()


def far_memory(count):
    return [pl.BlockSpec(memory_space=pltpu.HBM)] * count


def per_device(
    far_adjoint,
    wavenumber,
    design_params,
    family,
    send_pick,
    arrive_pick,
    input_weight,
    hidden_weight,
    output_weight,
):
    row_count, column_count = family.shape
    cell_count = row_count * column_count
    bands = far_adjoint.shape[0]
    band_groups = lax.axis_size("freq")
    segment = cell_count // band_groups
    chunks = segment // CHUNK
    pair_rows = 2 * bands
    shards, slots = send_pick.shape[1:]
    directions = far_adjoint.shape[1]
    n_cells = lax.axis_size("cells")
    width = 256 if slots % 256 == 0 else 128
    bf16, dma = jnp.bfloat16, pltpu.SemaphoreType.DMA
    last_weight = output_weight.reshape(NFAM, band_groups, pair_rows, HID)
    last_weight = jnp.pad(last_weight, ((0, 0), (0, 0), (0, SUB - pair_rows), (0, 0)))
    last_weight = last_weight.reshape(NFAM, band_groups * SUB, HID)
    input_weight = jnp.swapaxes(input_weight, 1, 2)
    return pl.pallas_call(
        functools.partial(fused_kernel, width=width),
        out_shape=pltpu.VMEM(design_params.shape, jnp.float32),
        in_specs=far_memory(9),
        out_specs=pl.BlockSpec(memory_space=pltpu.VMEM),
        scratch_shapes=[
            pltpu.SMEM(wavenumber.shape, jnp.float32),
            pltpu.VMEM(family.shape, jnp.int32),
            pltpu.VMEM((shards, slots), jnp.int32),
            pltpu.VMEM(arrive_pick.shape, jnp.int32),
            pltpu.VMEM(design_params.shape, bf16),
            pltpu.VMEM(input_weight.shape, bf16),
            pltpu.VMEM(hidden_weight.shape, bf16),
            pltpu.VMEM(last_weight.shape, bf16),
            dma((10,)),
            pltpu.VMEM((n_cells, bands, 2 * directions, V), bf16),
            pltpu.VMEM((bands, V, 2 * column_count), bf16),
            pltpu.VMEM((bands, 2 * row_count, 4 * U), bf16),
            pltpu.VMEM((pair_rows * row_count, column_count), bf16),
            pltpu.VMEM((row_count * SUB, column_count), bf16),
            pltpu.VMEM((shards, SUB, slots), bf16),
            pltpu.VMEM((shards, SUB, slots), bf16),
            pltpu.VMEM((shards * slots // width * SUB, width), jnp.float32),
            pltpu.VMEM((2, band_groups, SUB, segment), bf16),
            pltpu.VMEM((band_groups * SUB, segment), bf16),
            pltpu.VMEM((NFAM, 128), jnp.float32),
            pltpu.VMEM((shards, NFAM, 128), jnp.float32),
            pltpu.VMEM((1, 128), jnp.int32),
            pltpu.SMEM((1, 128), jnp.int32),
            pltpu.VMEM((NL + 1, segment, HID), bf16),
            dma((n_cells,)),
            dma((n_cells,)),
            dma((n_cells,)),
            dma((n_cells,)),
            dma((shards,)),
            dma((shards,)),
            dma((shards,)),
            dma((shards,)),
            dma((band_groups, chunks)),
            dma((band_groups, chunks)),
        ],
        compiler_params=pltpu.CompilerParams(
            collective_id=0, has_side_effects=True, vmem_limit_bytes=62 << 20
        ),
        name="fused",
    )(
        wavenumber,
        far_adjoint.reshape(bands, 2 * directions, V),
        family,
        send_pick.reshape(shards, slots),
        arrive_pick,
        design_params,
        input_weight,
        hidden_weight,
        last_weight,
    )


def solution(mesh):
    return jax.shard_map(
        per_device,
        mesh=mesh,
        in_specs=(
            P(("groups", "freq"), "cells", None, None),
            P("freq"),
            P(None, ("groups", "cells", "freq", "rep")),
            P(("groups", "cells"), "rep"),
            P(("groups", "cells", "rep"), None, None),
            P(("groups", "cells", "rep"), None),
            P(),
            P(),
            P(),
        ),
        out_specs=P(None, ("groups", "cells", "freq", "rep")),
        check_vma=False,
    )
```

```python
import functools
import math

import jax
import jax.numpy as jnp
from jax import lax
from jax.experimental import pallas as pl
from jax.experimental.pallas import tpu as pltpu
from jax.sharding import PartitionSpec as P

U = 128
V = 128
HID = 256
NL = 5
BLK = 128
NFAM = 8
SUB = 8
CHUNK = 1024
GRAIN = 512
UNROLL = 8


def one_hot_pick(table, index, width):
    count = index.shape[1]
    low = jnp.bitwise_and(index, width - 1).astype(jnp.float32).astype(jnp.bfloat16)
    high = jnp.right_shift(index, width.bit_length() - 1)
    level = lax.broadcasted_iota(jnp.int32, (width, count), 0)
    level = level.astype(jnp.float32).astype(jnp.bfloat16)
    one, zero = jnp.ones((), jnp.bfloat16), jnp.zeros((), jnp.bfloat16)
    chosen = jnp.where(level == jnp.broadcast_to(low, level.shape), one, zero)
    spread = jnp.dot(table, chosen, preferred_element_type=jnp.float32)
    high = jnp.broadcast_to(high, (SUB, count))
    total = jnp.zeros((SUB, count), jnp.float32)
    for step in range(table.shape[0] // SUB):
        total = jnp.where(high == step, spread[step * SUB : (step + 1) * SUB], total)
    return total


def row_order(pair_rows, row_count):
    shape = (row_count * SUB, pair_rows * row_count)
    target = lax.broadcasted_iota(jnp.int32, shape, 0)
    source = lax.broadcasted_iota(jnp.int32, shape, 1)
    wanted = (target % SUB) * row_count + target // SUB
    hit = jnp.logical_and(wanted == source, target % SUB < pair_rows)
    return jnp.where(hit, 1.0, 0.0).astype(jnp.bfloat16)


def angles_of(wavenumber, direction, position):
    return (wavenumber * direction) * position


def fill_right_tables(right_ref, wave_ref, column_start, column_count, column_total):
    group = 16
    scale = 1.0 / math.sqrt(V)
    for band in range(right_ref.shape[0]):
        wavenumber = wave_ref[band]
        for start in range(0, column_count, 128):
            column = lax.broadcasted_iota(jnp.int32, (group, 128), 1) + (column_start + start)
            position = column.astype(jnp.float32) - 0.5 * (column_total - 1)
            row = lax.broadcasted_iota(jnp.int32, (group, 128), 0).astype(jnp.float32)
            angle = angles_of(wavenumber, (2.0 * row + 1.0) / V - 1.0, position)
            cosine, sine = jnp.cos(angle) * scale, jnp.sin(angle) * scale
            turn = angles_of(wavenumber, 2.0 * group / V, position[:8])
            turn_cos, turn_sin = jnp.cos(turn), jnp.sin(turn)
            turn_cos = jnp.concatenate([turn_cos, turn_cos], 0)
            turn_sin = jnp.concatenate([turn_sin, turn_sin], 0)
            for low in range(0, V, group):
                at = pl.ds(low, group)
                right_ref[band, at, pl.ds(start, 128)] = cosine.astype(jnp.bfloat16)
                right_ref[band, at, pl.ds(column_count + start, 128)] = sine.astype(jnp.bfloat16)
                cosine, sine = (
                    cosine * turn_cos - sine * turn_sin,
                    sine * turn_cos + cosine * turn_sin,
                )


def fill_left_tables(left_ref, wave_ref, row_start, row_count, rows_total):
    scale = 1.0 / math.sqrt(U)
    shape = (row_count, 2 * U)
    row = lax.broadcasted_iota(jnp.int32, shape, 0) + row_start
    position = row.astype(jnp.float32) - 0.5 * (rows_total - 1)
    lane = lax.broadcasted_iota(jnp.int32, shape, 1)
    direction = (2.0 * (lane // 2).astype(jnp.float32) + 1.0) / U - 1.0
    real = lane % 2 == 0
    for band in range(left_ref.shape[0]):
        angle = angles_of(wave_ref[band], direction, position)
        cosine, sine = jnp.cos(angle) * scale, jnp.sin(angle) * scale
        upper = jnp.where(real, cosine, -sine).astype(jnp.bfloat16)
        lower = jnp.where(real, sine, cosine).astype(jnp.bfloat16)
        left_ref[band, :row_count, : 2 * U] = upper
        left_ref[band, row_count:, : 2 * U] = lower
        left_ref[band, :row_count, 2 * U :] = -lower
        left_ref[band, row_count:, 2 * U :] = upper


def nt_dot(left, right):
    return lax.dot_general(
        left, right, (((1,), (1,)), ((), ())), preferred_element_type=jnp.float32
    )


def tn_dot(left, right):
    return lax.dot_general(
        left, right, (((0,), (0,)), ((), ())), preferred_element_type=jnp.float32
    )


def blocks_of(chunk, kind_ref):
    first = chunk * (CHUNK // BLK)
    return [
        (
            pl.ds(pl.multiple_of((first + i) * BLK, BLK), BLK),
            jnp.clip(kind_ref[0, first + i], 0, NFAM - 1),
        )
        for i in range(CHUNK // BLK)
    ]


def forward_chunk(chunk, kind_ref, inputs_ref, first_ref, hidden_ref, slope_ref):
    half = jnp.asarray(0.5, jnp.bfloat16)
    blocks = blocks_of(chunk, kind_ref)
    preacts = [tn_dot(inputs_ref[:, at] * half, first_ref[kind]) for at, kind in blocks]
    for level in range(NL + 1):
        for place, (at, kind) in enumerate(blocks):
            above = 1.0 + jnp.tanh(preacts[place])
            active = preacts[place] * above
            above, active = above.astype(jnp.bfloat16), active.astype(jnp.bfloat16)
            slope_ref[level, at] = above + active * (2.0 - above)
            if level < NL:
                preacts[place] = nt_dot(active, hidden_ref[kind, level])


def backward_chunk(chunk, kind_ref, ordered_ref, first_ref, hidden_ref, last_ref, slope_ref, out_ref):
    blocks = blocks_of(chunk, kind_ref)

    def delta_of(level, place, at):
        slope = slope_ref[level, at].astype(jnp.float32)
        return (gradients[place] * slope).astype(jnp.bfloat16)

    gradients = [tn_dot(ordered_ref[:, at], last_ref[kind]) for at, kind in blocks]
    for level in reversed(range(NL)):
        for place, (at, kind) in enumerate(blocks):
            gradients[place] = jnp.dot(
                delta_of(level + 1, place, at),
                hidden_ref[kind, level],
                preferred_element_type=jnp.float32,
            )
    for place, (at, kind) in enumerate(blocks):
        out_ref[:, at] = nt_dot(first_ref[kind], delta_of(0, place, at)) * 0.5


def fused_kernel(
    wave_hbm,
    far_ref,
    family_hbm,
    send_hbm,
    arrive_hbm,
    inputs_hbm,
    first_hbm,
    hidden_hbm,
    last_hbm,
    result_ref,
    wave_ref,
    family_ref,
    send_ref,
    arrive_ref,
    inputs_ref,
    first_ref,
    hidden_ref,
    last_ref,
    load_sem,
    field_ref,
    right_ref,
    left_ref,
    image_ref,
    cells_ref,
    table_ref,
    outbox_ref,
    got_ref,
    gather_ref,
    half_ref,
    ordered_ref,
    count_ref,
    counts_ref,
    kind_vmem,
    kind_ref,
    slope_ref,
    far_send,
    far_recv,
    pass_send,
    pass_recv,
    count_send,
    count_recv,
    out_send,
    out_recv,
    half_send,
    half_recv,
    *,
    width,
):
    n_cells, n_rep, n_freq = (lax.axis_size(name) for name in ("cells", "rep", "freq"))
    z, core, freq = (lax.axis_index(name) for name in ("cells", "rep", "freq"))
    shards = n_cells * n_rep
    me = z * n_rep + core
    bands = far_ref.shape[0]
    row_count, column_count = family_ref.shape
    slots = send_ref.shape[1]
    segment = ordered_ref.shape[1]
    pair_rows = 2 * bands
    share = bands // n_rep
    chunks = segment // CHUNK
    mesh_ids = pl.DeviceIdType.MESH

    def shard_id(shard):
        return {"cells": shard // n_rep, "rep": shard % n_rep}

    def partner(own, mask, count):
        other, bit = 0, 1
        while bit < count:
            mine, flip = (own // bit) % 2, (mask // bit) % 2
            other, bit = other + bit * (mine + flip - 2 * mine * flip), 2 * bit
        return other

    loads = [
        pltpu.make_async_copy(source, target, load_sem.at[place])
        for place, (source, target) in enumerate(
            (
                (wave_hbm, wave_ref),
                (family_hbm, family_ref),
                (far_ref, field_ref.at[z]),
                (send_hbm, send_ref),
                (inputs_hbm, inputs_ref),
                (first_hbm, first_ref),
                (hidden_hbm, hidden_ref),
                (last_hbm, last_ref),
                (arrive_hbm, arrive_ref),
            )
        )
    ]
    for load in loads[:2]:
        load.start()

    barrier = pltpu.get_barrier_semaphore()

    @pl.loop(1, shards)
    def _(step):
        pl.semaphore_signal(
            barrier, inc=1, device_id=shard_id((me + step) % shards), device_id_type=mesh_ids
        )

    @pl.loop(1, n_freq)
    def _(step):
        pl.semaphore_signal(
            barrier, inc=1, device_id={"freq": (freq + step) % n_freq}, device_id_type=mesh_ids
        )

    for load in loads[2:]:
        load.start()
    for load in loads[:2]:
        load.wait()

    rows = []
    for kind in range(NFAM):
        below = jnp.where(family_ref[...] <= kind, 1.0, 0.0)
        part = jnp.sum(below, 0, keepdims=True)
        total = part[:, :128]
        for start in range(128, column_count, 128):
            total = total + part[:, start : start + 128]
        rows.append(total)
    count_ref[...] = jnp.concatenate(rows, 0)
    counts_ref[me] = count_ref[...]

    pl.semaphore_wait(barrier, shards - 1 + n_freq - 1)

    def far_copy(mask):
        mine = pl.ds(core * share, share)
        return pltpu.make_async_remote_copy(
            src_ref=far_ref.at[mine],
            dst_ref=field_ref.at[z, mine],
            send_sem=far_send.at[mask],
            recv_sem=far_recv.at[mask],
            device_id={"cells": partner(z, mask, n_cells)},
            device_id_type=mesh_ids,
        )

    def far_arrival(mask):
        mine = pl.ds(core * share, share)
        source = partner(z, mask, n_cells)
        return pltpu.make_async_remote_copy(
            src_ref=far_ref.at[mine],
            dst_ref=field_ref.at[source, mine],
            send_sem=far_send.at[mask],
            recv_sem=far_recv.at[mask],
            device_id={"cells": source},
            device_id_type=mesh_ids,
        )

    def pass_copy(mask, lane):
        mine = pl.ds(lane * share, share)
        source = partner(z, mask, n_cells)
        return pltpu.make_async_remote_copy(
            src_ref=field_ref.at[source, mine],
            dst_ref=field_ref.at[source, mine],
            send_sem=pass_send.at[mask],
            recv_sem=pass_recv.at[mask],
            device_id={"rep": 1 - core},
            device_id_type=mesh_ids,
        )

    def count_copy(step, shard, slot):
        return pltpu.make_async_remote_copy(
            src_ref=count_ref,
            dst_ref=counts_ref.at[slot],
            send_sem=count_send.at[step],
            recv_sem=count_recv.at[slot],
            device_id=shard_id(shard),
            device_id_type=mesh_ids,
        )

    @pl.loop(1, shards)
    def _(step):
        count_copy(step, (me + step) % shards, me).start()

    for mask in reversed(range(1, n_cells)):
        far_copy(mask).start()

    fill_right_tables(right_ref, wave_ref, core * column_count, column_count, column_count * n_rep)
    fill_left_tables(left_ref, wave_ref, z * row_count, row_count, row_count * n_cells)

    for load in loads[2:]:
        load.wait()

    @pl.loop(0, NFAM)
    def _(kind):
        for level in range(NL):
            hidden_ref[kind, level] = hidden_ref[kind, level] * jnp.asarray(0.5, jnp.bfloat16)

    def image_of(source):
        for band in range(bands):
            image = jnp.dot(
                field_ref[source, band], right_ref[band], preferred_element_type=jnp.float32
            ).astype(jnp.bfloat16)
            image_ref[band, 0, source] = image[:, :column_count]
            image_ref[band, 1, source] = image[:, column_count:]

    image_of(z)

    @pl.loop(1, shards)
    def _(step):
        count_copy(step, (me + step) % shards, (me + step) % shards).wait_recv()

    upto = jnp.sum(jnp.sum(counts_ref[...], 0), 1, keepdims=True)
    owner = (z * n_freq + freq) * n_rep + core
    block = lax.broadcasted_iota(jnp.int32, (NFAM, 128), 1)
    level = lax.broadcasted_iota(jnp.int32, (NFAM, 128), 0)
    position = (owner * segment + block * BLK).astype(jnp.float32)
    past = jnp.where(jnp.logical_and(position >= upto, level < NFAM - 1), 1.0, 0.0)
    kind_vmem[...] = jnp.sum(past, 0, keepdims=True).astype(jnp.int32)
    kind_load = pltpu.make_async_copy(kind_vmem, kind_ref, load_sem.at[len(loads)])
    kind_load.start()
    kind_load.wait()

    def forward(chunk):
        forward_chunk(chunk, kind_ref, inputs_ref, first_ref, hidden_ref, slope_ref)

    early, last_chunks = 1, chunks // 4

    for mask in range(1, n_cells):
        far_arrival(mask).wait_recv()
        pass_copy(mask, core).start()
        if mask == 1:
            pl.loop(0, early)(forward)
    for mask in range(1, n_cells):
        pass_copy(mask, 1 - core).wait_recv()
        image_of(partner(z, mask, n_cells))

    for band in range(bands):
        stacked = image_ref[band].reshape(4 * U, column_count)
        cells_ref[band * 2 * row_count : (band + 1) * 2 * row_count] = jnp.dot(
            left_ref[band], stacked, preferred_element_type=jnp.float32
        ).astype(jnp.bfloat16)
    table_ref[...] = jnp.dot(
        row_order(pair_rows, row_count), cells_ref[...], preferred_element_type=jnp.float32
    ).astype(jnp.bfloat16)

    def out_copy(shard, slot):
        return pltpu.make_async_remote_copy(
            src_ref=outbox_ref.at[shard],
            dst_ref=got_ref.at[slot],
            send_sem=out_send.at[shard],
            recv_sem=out_recv.at[slot],
            device_id=shard_id(shard),
            device_id_type=mesh_ids,
        )

    grain = GRAIN if slots % GRAIN == 0 else slots

    def send_picked(step):
        shard = partner(me, shards - step, shards)
        for start in range(0, slots, grain):
            at = pl.ds(start, grain)
            picked = one_hot_pick(table_ref[...], send_ref[pl.ds(shard, 1), at], column_count)
            outbox_ref[shard, :, at] = picked.astype(jnp.bfloat16)
        out_copy(shard, me).start()

    if shards <= UNROLL:
        for step in range(1, shards):
            send_picked(step)
    else:
        pl.loop(1, shards)(send_picked)

    for start in range(0, slots, grain):
        at = pl.ds(start, grain)
        picked = one_hot_pick(table_ref[...], send_ref[pl.ds(me, 1), at], column_count)
        got_ref[me, :, at] = picked.astype(jnp.bfloat16)

    pl.loop(early, chunks - last_chunks)(forward)

    @pl.loop(1, shards)
    def _(step):
        shard = (me + step) % shards
        out_copy(shard, shard).wait_recv()

    per_shard = slots // width
    for shard in range(shards):
        for part in range(per_shard):
            row = (shard * per_shard + part) * SUB
            gather_ref[row : row + SUB] = got_ref[
                shard, :, part * width : (part + 1) * width
            ].astype(jnp.float32)
    gathered = gather_ref[...].astype(jnp.bfloat16)

    def half_copy(step, slot, chunk):
        at = pl.ds(pl.multiple_of(chunk * CHUNK, CHUNK), CHUNK)
        return pltpu.make_async_remote_copy(
            src_ref=half_ref.at[0, step, :, at],
            dst_ref=half_ref.at[1, slot, :, at],
            send_sem=half_send.at[step, chunk],
            recv_sem=half_recv.at[slot, chunk],
            device_id={"freq": (freq + step) % n_freq},
            device_id_type=mesh_ids,
        )

    piece = 512

    def pick_half(target, chunk, side, slot):
        for start in range(chunk * CHUNK, (chunk + 1) * CHUNK, piece):
            at = pl.ds(pl.multiple_of(target * segment + start, piece), piece)
            half_ref[side, slot, :, pl.ds(start, piece)] = one_hot_pick(
                gathered, arrive_ref[:, at], width
            ).astype(jnp.bfloat16)

    @pl.loop(1, n_freq)
    def _(step):
        for chunk in range(chunks):
            pick_half((freq + step) % n_freq, chunk, 0, step)
            half_copy(step, freq, chunk).start()

    for chunk in range(chunks):
        pick_half(freq, chunk, 1, freq)

    pl.loop(chunks - last_chunks, chunks)(forward)

    def columns(chunk):
        return pl.ds(pl.multiple_of(chunk * CHUNK, CHUNK), CHUNK)

    def backward(chunk):
        @pl.loop(1, n_freq)
        def _(step):
            half_copy(step, (freq + step) % n_freq, chunk).wait_recv()

        for group in range(n_freq):
            ordered_ref[group * SUB : (group + 1) * SUB, columns(chunk)] = half_ref[
                1, group, :, columns(chunk)
            ]
        backward_chunk(
            chunk, kind_ref, ordered_ref, first_ref, hidden_ref, last_ref, slope_ref, result_ref
        )

    @pl.loop(0, chunks // 2)
    def _(pair):
        backward(2 * pair)
        backward(2 * pair + 1)

    for mask in range(1, n_cells):
        far_copy(mask).wait_send()
        pass_copy(mask, core).wait_send()

    @pl.loop(1, shards)
    def _(step):
        count_copy(step, (me + step) % shards, me).wait_send()
        out_copy((me + step) % shards, me).wait_send()

    @pl.loop(1, n_freq)
    def _(step):
        for chunk in range(chunks):
            half_copy(step, freq, chunk).wait_send()


def far_memory(count):
    return [pl.BlockSpec(memory_space=pltpu.HBM)] * count


def per_device(
    far_adjoint,
    wavenumber,
    design_params,
    family,
    send_pick,
    arrive_pick,
    input_weight,
    hidden_weight,
    output_weight,
):
    row_count, column_count = family.shape
    cell_count = row_count * column_count
    bands = far_adjoint.shape[0]
    band_groups = lax.axis_size("freq")
    segment = cell_count // band_groups
    chunks = segment // CHUNK
    pair_rows = 2 * bands
    shards, slots = send_pick.shape[1:]
    directions = far_adjoint.shape[1]
    n_cells = lax.axis_size("cells")
    width = 256 if slots % 256 == 0 else 128
    bf16, dma = jnp.bfloat16, pltpu.SemaphoreType.DMA
    last_weight = output_weight.reshape(NFAM, band_groups, pair_rows, HID)
    last_weight = jnp.pad(last_weight, ((0, 0), (0, 0), (0, SUB - pair_rows), (0, 0)))
    last_weight = last_weight.reshape(NFAM, band_groups * SUB, HID)
    input_weight = jnp.swapaxes(input_weight, 1, 2)
    return pl.pallas_call(
        functools.partial(fused_kernel, width=width),
        out_shape=pltpu.VMEM(design_params.shape, jnp.float32),
        in_specs=far_memory(9),
        out_specs=pl.BlockSpec(memory_space=pltpu.VMEM),
        scratch_shapes=[
            pltpu.SMEM(wavenumber.shape, jnp.float32),
            pltpu.VMEM(family.shape, jnp.int32),
            pltpu.VMEM((shards, slots), jnp.int32),
            pltpu.VMEM(arrive_pick.shape, jnp.int32),
            pltpu.VMEM(design_params.shape, bf16),
            pltpu.VMEM(input_weight.shape, bf16),
            pltpu.VMEM(hidden_weight.shape, bf16),
            pltpu.VMEM(last_weight.shape, bf16),
            dma((10,)),
            pltpu.VMEM((n_cells, bands, 2 * directions, V), bf16),
            pltpu.VMEM((bands, V, 2 * column_count), bf16),
            pltpu.VMEM((bands, 2 * row_count, 4 * U), bf16),
            pltpu.VMEM((bands, 2, n_cells, 2 * directions, column_count), bf16),
            pltpu.VMEM((pair_rows * row_count, column_count), bf16),
            pltpu.VMEM((row_count * SUB, column_count), bf16),
            pltpu.VMEM((shards, SUB, slots), bf16),
            pltpu.VMEM((shards, SUB, slots), bf16),
            pltpu.VMEM((shards * slots // width * SUB, width), jnp.float32),
            pltpu.VMEM((2, band_groups, SUB, segment), bf16),
            pltpu.VMEM((band_groups * SUB, segment), bf16),
            pltpu.VMEM((NFAM, 128), jnp.float32),
            pltpu.VMEM((shards, NFAM, 128), jnp.float32),
            pltpu.VMEM((1, 128), jnp.int32),
            pltpu.SMEM((1, 128), jnp.int32),
            pltpu.VMEM((NL + 1, segment, HID), bf16),
            dma((n_cells,)),
            dma((n_cells,)),
            dma((n_cells,)),
            dma((n_cells,)),
            dma((shards,)),
            dma((shards,)),
            dma((shards,)),
            dma((shards,)),
            dma((band_groups, chunks)),
            dma((band_groups, chunks)),
        ],
        compiler_params=pltpu.CompilerParams(
            collective_id=0, has_side_effects=True, vmem_limit_bytes=62 << 20
        ),
        name="fused",
    )(
        wavenumber,
        far_adjoint.reshape(bands, 2 * directions, V),
        family,
        send_pick.reshape(shards, slots),
        arrive_pick,
        design_params,
        input_weight,
        hidden_weight,
        last_weight,
    )


def solution(mesh):
    return jax.shard_map(
        per_device,
        mesh=mesh,
        in_specs=(
            P(("groups", "freq"), "cells", None, None),
            P("freq"),
            P(None, ("groups", "cells", "freq", "rep")),
            P(("groups", "cells"), "rep"),
            P(("groups", "cells", "rep"), None, None),
            P(("groups", "cells", "rep"), None),
            P(),
            P(),
            P(),
        ),
        out_specs=P(None, ("groups", "cells", "freq", "rep")),
        check_vma=False,
    )
```
